512 devices in a mesh: term: 16 (over z), doc: 32 (over x, y, core).
Axes of the slice: x: 4, y: 4, z: 16, core: 2. Of those that a mesh axis runs over, the one named last changes fastest.
Arguments:
- postings: bfloat16 [16384, 30720], P('doc', 'term'), may hold values from 0 to 3
- query_terms: int32 [128, 32], replicated, may hold values from 0 to 30719
- query_levels: int32 [128, 32], replicated, may hold values from 1 to 255
- feedback_ids: int32 [128, 10], replicated, may hold values from 0 to 16383, as said below
Outputs:
- first_scores: float32 [128, 16384], P('term', 'doc')
- final_scores: float32 [128, 16384], P('term', 'doc')
The draws below stay inside these ranges and needn't reach their ends.
Inputs may be any that keep to these rules, and one draw needn't show every extreme that they name: `feedback_ids`: the 1280 feedback ids are all different.
All inputs are finite; a program needn't handle non-finite values.
Results may differ from the reference program's by a relative error of at most 0.0015.
Values may be sent and summed in bfloat16 or wider, within the bound.
No kernel may reach another device: no remote copies, remote signals or barrier semaphores. Data moves between devices by JAX's collectives and lax.ppermute only.
A program may use at most 64 MiB of HBM per device.

```python
import math
import jax
import jax.numpy as jnp
from jax import lax

VOCAB = 30720
Q = 128
QT = 32
FB = 10
TOPICS = 256
DOCS = 16384


background_share = 0.004


def topic_tables(key):
    term_order = jax.random.permutation(jax.random.fold_in(key, 101), VOCAB).astype(jnp.int32)
    term_positions = jnp.arange(VOCAB, dtype=jnp.int32)
    term_topic = jnp.zeros((VOCAB,), jnp.int32).at[term_order].set(term_positions % TOPICS)
    query_topic = jax.random.randint(jax.random.fold_in(key, 102), (Q,), 0, TOPICS, dtype=jnp.int32)
    shuffled = jax.random.permutation(jax.random.fold_in(key, 103), DOCS).astype(jnp.int32)
    at_ends = (shuffled == 0) | (shuffled == DOCS - 1)
    rank_keys = jnp.where(at_ends, -1, jnp.arange(DOCS, dtype=jnp.int32))
    picked = shuffled[jnp.argsort(rank_keys, stable=True)][:Q * FB]
    picked = jax.random.permutation(jax.random.fold_in(key, 104), picked)
    feedback_ids = picked.reshape(Q, FB)
    base_topic = jax.random.randint(jax.random.fold_in(key, 105), (DOCS,), 0, TOPICS, dtype=jnp.int32)
    passage_topic = base_topic.at[picked].set(jnp.repeat(query_topic, FB))
    return (term_order, term_topic, query_topic, feedback_ids, passage_topic)


def draw_postings(key, part):
    term_order, term_topic, query_topic, feedback_ids, passage_topic = topic_tables(key)
    uniform_draw = jax.random.uniform(jax.random.fold_in(key, 106), (DOCS, VOCAB), jnp.float32)
    core_mask = passage_topic[:, None] == term_topic[None, :]
    spare_mask = uniform_draw < background_share
    spare_level = uniform_draw / background_share
    core_value = 0.1 * jnp.exp(uniform_draw * math.log(30.0))
    spare_value = 0.02 * jnp.exp(spare_level * math.log(50.0))
    weights = jnp.where(core_mask, core_value, jnp.where(spare_mask, spare_value, 0.0))
    return weights.astype(jnp.bfloat16)


def draw_query_terms(key, part):
    term_order, term_topic, query_topic, feedback_ids, passage_topic = topic_tables(key)
    core_slots = QT // 2
    slot_picks = jax.random.randint(jax.random.fold_in(key, 107), (Q, core_slots), 0, VOCAB // TOPICS, dtype=jnp.int32)
    core_terms = term_order[query_topic[:, None] + TOPICS * slot_picks]
    other_terms = jax.random.randint(jax.random.fold_in(key, 108), (Q, QT - core_slots), 0, VOCAB, dtype=jnp.int32)
    low_row = jax.random.randint(jax.random.fold_in(key, 109), (), 0, Q, dtype=jnp.int32)
    high_row = jax.random.randint(jax.random.fold_in(key, 110), (), 0, Q, dtype=jnp.int32)
    other_terms = other_terms.at[low_row, 0].set(0).at[high_row, 1].set(VOCAB - 1)
    all_slots = jnp.concatenate([core_terms, other_terms], axis=1)
    return jax.random.permutation(jax.random.fold_in(key, 111), all_slots, axis=1, independent=True)


def draw_feedback_ids(key, part):
    term_order, term_topic, query_topic, feedback_ids, passage_topic = topic_tables(key)
    return feedback_ids


def touch_ends(values, stream_key, smallest, top_value):
    spot = [jax.random.randint(jax.random.fold_in(stream_key, axis), (), 0, length) for axis, length in enumerate(values.shape)]
    longest = values.shape.index(max(values.shape))
    next_to = spot[:longest] + [(spot[longest] + 1) % values.shape[longest]] + spot[longest + 1:]
    return values.at[tuple(spot)].set(smallest).at[tuple(next_to)].set(top_value)


def setup_inputs(seed: int = 0) -> dict:
    streams_of = jax.random.split(jax.random.key(seed), 5)
    return {
        "postings": draw_postings(jax.random.fold_in(streams_of[4], 71), 0),
        "query_terms": draw_query_terms(jax.random.fold_in(streams_of[4], 71), 0),
        "query_levels": touch_ends(jax.random.randint(streams_of[2], (Q, QT), 1, 256), jax.random.fold_in(streams_of[2], 1), 1, 255).astype(jnp.int32),
        "feedback_ids": draw_feedback_ids(jax.random.fold_in(streams_of[4], 71), 0),
    }


expansion_weight = 0.25


def score_all(query_rows, postings):
    return lax.dot_general(query_rows, postings, (((1,), (1,)), ((), ())), preferred_element_type=jnp.float32)


def reference(postings, query_terms, query_levels, feedback_ids):
    queries = query_terms.shape[0]
    row_index = jnp.broadcast_to(jnp.arange(queries, dtype=jnp.int32)[:, None], query_terms.shape)
    query_vector = jnp.zeros((queries, VOCAB), jnp.float32).at[row_index, query_terms].add(query_levels.astype(jnp.float32) / 100.0)
    first_scores = score_all(query_vector.astype(jnp.bfloat16), postings)
    feedback = jnp.take_along_axis(first_scores, feedback_ids, axis=1).astype(jnp.bfloat16)
    feedback_rows = jnp.broadcast_to(jnp.arange(queries, dtype=jnp.int32)[:, None], feedback_ids.shape)
    mixing = jnp.zeros((queries, DOCS), jnp.float32).at[feedback_rows, feedback_ids].add(feedback.astype(jnp.float32)).astype(jnp.bfloat16)
    numerator = jnp.dot(mixing, postings, preferred_element_type=jnp.float32)
    weight_sum = jnp.sum(feedback.astype(jnp.float32), axis=1)
    expanded = (query_vector + expansion_weight * numerator / weight_sum[:, None]).astype(jnp.bfloat16)
    final_scores = score_all(expanded, postings)
    return first_scores, final_scores
```

```python
import jax
import jax.numpy as jnp
from jax import lax
from jax.sharding import PartitionSpec as P

expansion_weight = 0.25


def query_slice(query_terms, query_levels, width, offset):
    columns = offset + lax.iota(jnp.int32, width)
    total = jnp.zeros((query_terms.shape[0], width), jnp.int32)
    for k in range(query_terms.shape[1]):
        hit = query_terms[:, k : k + 1] == columns[None, :]
        total = total + jnp.where(hit, query_levels[:, k : k + 1], 0)
    return total.astype(jnp.float32) / 100.0


def score_block(query_rows, postings):
    return lax.dot_general(
        query_rows, postings, (((1,), (1,)), ((), ())), preferred_element_type=jnp.float32
    )


def per_device(postings, query_terms, query_levels, feedback_ids):
    doc_rows, width = postings.shape
    queries = query_terms.shape[0]
    terms = lax.axis_size("term")
    docs = lax.axis_size("doc")
    group = queries // terms
    chunk = queries // docs
    term_index = lax.axis_index("term")
    doc_index = lax.axis_index("doc")
    query_part = query_slice(query_terms, query_levels, width, term_index * width)
    partial = score_block(query_part.astype(jnp.bfloat16), postings)

    positions = doc_index * doc_rows + lax.iota(jnp.int32, doc_rows)
    member = jnp.zeros((queries, doc_rows), jnp.bool_)
    for j in range(feedback_ids.shape[1]):
        member = member | (feedback_ids[:, j : j + 1] == positions[None, :])
    chosen = jnp.sum(jnp.where(member, partial, 0.0), axis=0)

    chosen_all = lax.all_to_all(
        jnp.broadcast_to(chosen.reshape(1, 4, doc_rows // 4), (terms, 4, doc_rows // 4)), "term", 0, 0
    )
    weight = jnp.sum(chosen_all, axis=0).reshape(doc_rows).astype(jnp.bfloat16)
    mixing = jnp.where(member, weight[None, :], jnp.zeros((), jnp.bfloat16))
    numerator = jnp.dot(mixing, postings, preferred_element_type=jnp.float32)
    weight_part = jnp.sum(mixing.astype(jnp.float32), axis=1, keepdims=True)
    high = weight_part.astype(jnp.bfloat16).astype(jnp.float32)
    pair = jnp.concatenate([high, weight_part - high], axis=1)
    pair = jnp.pad(pair, ((0, 0), (0, 126)))
    packed = jnp.concatenate([numerator, pair], axis=1).astype(jnp.bfloat16)
    shares = lax.all_to_all(packed.reshape(docs, chunk, width + 128), "doc", 0, 0)
    total = jnp.sum(shares.astype(jnp.float32), axis=0)
    weight_sum = total[:, width : width + 1] + total[:, width + 1 : width + 2]
    own = lax.dynamic_slice_in_dim(query_part, doc_index * chunk, chunk, 0)
    expanded_own = (own + expansion_weight * total[:, :width] / weight_sum).astype(jnp.bfloat16)
    expanded = lax.all_to_all(
        jnp.broadcast_to(expanded_own[None], (docs, chunk, width)), "doc", 0, 0
    ).reshape(queries, width)
    final = score_block(expanded, postings)
    both = jnp.stack([partial.reshape(terms, group, doc_rows), final.reshape(terms, group, doc_rows)], axis=1)
    both = both.astype(jnp.bfloat16).reshape(terms, 2 * group, doc_rows)
    sums = jnp.sum(lax.all_to_all(both, "term", 0, 0).astype(jnp.float32), axis=0)
    return (sums[:group], sums[group:])


def solution(mesh):
    return jax.shard_map(
        per_device,
        mesh=mesh,
        in_specs=(P("doc", "term"), P(), P(), P()),
        out_specs=(P("term", "doc"), P("term", "doc")),
        check_vma=False,
    )
```

```python
import jax
import jax.numpy as jnp
from jax import lax
from jax.experimental import pallas as pl
from jax.experimental.pallas import tpu as pltpu
from jax.sharding import PartitionSpec as P

expansion_weight = 0.25
lanes = 128
half = 1024
f32 = jnp.float32
bf16 = jnp.bfloat16
VMEM = pl.BlockSpec(memory_space=pltpu.VMEM)


def dot_nt(a, b):
    return lax.dot_general(a, b, (((1,), (1,)), ((), ())), preferred_element_type=f32)


def iota(shape, axis):
    return lax.broadcasted_iota(jnp.int32, shape, axis)


def first_round(terms_ref, levels_ref, ids_ref, postings_hbm, send_ref, mask_ref, query_ref,
                postings_ref, sem):
    copy = pltpu.make_async_copy(postings_hbm, postings_ref, sem)
    copy.start()
    slots, queries = terms_ref.shape
    docs, width = postings_ref.shape
    tiles = width // lanes
    spread = 8 * slots
    local = terms_ref[...] - lax.axis_index("term") * width
    tile_of = lax.shift_right_arithmetic(local, 7)
    lane_of = local & 127
    repeat = (iota((slots, spread), 0) == (iota((slots, spread), 1) & (slots - 1))).astype(f32).astype(bf16)
    stacked = jnp.concatenate([tile_of, lane_of, levels_ref[...]], axis=1).astype(f32).astype(bf16)
    wide = lax.dot_general(stacked, repeat, (((0,), (0,)), ((), ())), preferred_element_type=f32)
    own = lax.shift_right_logical(iota((8, spread), 1), 5) == iota((8, spread), 0)
    lane_ids = iota((lanes, spread), 0).astype(f32)
    for block in range(queries // 8):
        rows = slice(8 * block, 8 * block + 8)
        tile_now = wide[rows]
        lane_now = wide[queries + 8 * block : queries + 8 * block + 8]
        level_now = wide[2 * queries + 8 * block : 2 * queries + 8 * block + 8]
        lane_row = jnp.sum(jnp.where(own, lane_now, 0.0), axis=0, keepdims=True)
        level_own = jnp.where(own, level_now, 0.0)
        hot = jnp.where(lane_ids == lane_row, 1.0, 0.0).astype(bf16)
        parts = [jnp.where(tile_now == float(t), level_own, 0.0) for t in range(tiles)]
        totals = dot_nt(jnp.concatenate(parts, axis=0).astype(bf16), hot)
        for t in range(tiles):
            query_ref[rows, t * lanes : (t + 1) * lanes] = totals[8 * t : 8 * t + 8] * f32(0.01)
    place = iota((docs, queries), 0) + lax.axis_index("doc") * docs
    member = ids_ref[0:1, :] == place
    for j in range(1, ids_ref.shape[0]):
        member = member | (ids_ref[j : j + 1, :] == place)
    member = jnp.where(member, 1.0, 0.0).astype(bf16)
    wanted = iota((3 * queries, queries), 0)
    doubled = lax.shift_right_logical(wanted - queries, 3) * 4 + (wanted & 3)
    source = jnp.where(wanted < queries, wanted, doubled)
    pick = jnp.where(source == iota((3 * queries, queries), 1), 1.0, 0.0).astype(bf16)
    masks = dot_nt(pick, member)
    mask = masks[:queries]
    mask_ref[...] = masks[queries:].astype(bf16)
    copy.wait()
    scores = dot_nt(query_ref[...].astype(bf16), postings_ref[...])
    chosen = jnp.sum(scores * mask, axis=0, keepdims=True)
    high = chosen.astype(bf16).astype(f32)
    low = chosen - high
    steps = docs // lanes
    pieces = [x[:, i * lanes : (i + 1) * lanes] for x in (high, low) for i in range(steps)]
    tail = jnp.concatenate(pieces, axis=0).astype(bf16)
    for g in range(queries // 8):
        send_ref[g, :, 0:docs] = scores[8 * g : 8 * g + 8].astype(bf16)
        send_ref[g, :, docs : docs + lanes] = tail


def feedback_round(received_ref, mask_ref, postings_ref, first_ref, send_ref):
    groups = received_ref.shape[0]
    docs, width = postings_ref.shape
    total = received_ref[0].astype(f32)
    for g in range(1, groups):
        total = total + received_ref[g].astype(f32)
    first_ref[...] = total[:, 0:docs]
    steps = docs // lanes
    tail = total[:, docs : docs + lanes]
    weight = jnp.concatenate([tail[i : i + 1] + tail[steps + i : steps + i + 1] for i in range(steps)], axis=1)
    weight = weight.astype(bf16).astype(f32)
    mixing = (mask_ref[...].astype(f32) * weight).astype(bf16)
    postings = postings_ref[...]
    left = jnp.dot(mixing, postings[:, 0:half], preferred_element_type=f32)
    right = jnp.dot(mixing, postings[:, half:width], preferred_element_type=f32)
    sums = jnp.dot(mixing, jnp.ones((docs, lanes), bf16), preferred_element_type=f32)
    high = sums.astype(bf16).astype(f32)
    lane = iota(sums.shape, 1)
    sums = jnp.where(lane == 0, high, jnp.where(lane == 1, sums - high, 0.0))
    right = jnp.concatenate([right, sums], axis=1)
    upper = iota((8, half), 0) < 4
    for c in range(send_ref.shape[0]):
        rows = slice(8 * c, 8 * c + 8)
        send_ref[c] = jnp.where(upper, left[rows], right[rows]).astype(bf16)


def expand(received_ref, query_ref, out_ref):
    chunk, width = out_ref.shape
    total = received_ref[0].astype(f32)
    for d in range(1, received_ref.shape[0]):
        total = total + received_ref[d].astype(f32)
    rest = width - half
    weight = total[chunk:, rest : rest + 1] + total[chunk:, rest + 1 : rest + 2]
    doc = lax.axis_index("doc")
    pair = query_ref[pl.ds(pl.multiple_of(lax.shift_right_logical(doc, 1) * 8, 8), 8), :]
    mine = jnp.where((doc & 1) == 0, pair[:chunk], pair[chunk:])
    left = mine[:, :half] + expansion_weight * total[:chunk] / weight
    right = mine[:, half:] + expansion_weight * total[chunk:, :rest] / weight
    out_ref[:, 0:half] = left.astype(bf16)
    out_ref[:, half:width] = right.astype(bf16)


def per_device(postings, query_terms, query_levels, feedback_ids):
    docs, width = postings.shape
    queries = query_terms.shape[0]
    groups = lax.axis_size("term")
    blocks = lax.axis_size("doc")
    group = queries // groups
    chunk = queries // blocks
    shape = jax.ShapeDtypeStruct
    send, mask, query = pl.pallas_call(
        first_round,
        out_shape=(
            shape((groups, group, docs + lanes), bf16),
            shape((2 * queries, docs), bf16),
            shape((queries, width), f32),
        ),
        in_specs=[VMEM, VMEM, VMEM, pl.BlockSpec(memory_space=pltpu.HBM)],
        out_specs=(VMEM, VMEM, VMEM),
        scratch_shapes=[pltpu.VMEM((docs, width), bf16), pltpu.SemaphoreType.DMA],
        compiler_params=pltpu.CompilerParams(vmem_limit_bytes=32 << 20),
        name="first_round",
    )(query_terms.T, query_levels.T, feedback_ids.T, pltpu.with_memory_space_constraint(postings, pltpu.HBM))
    received = lax.all_to_all(send, "term", 0, 0)
    first, send = pl.pallas_call(
        feedback_round,
        out_shape=(shape((group, docs), f32), shape((blocks, 8, half), bf16)),
        in_specs=[VMEM] * 3,
        out_specs=(VMEM, VMEM),
        compiler_params=pltpu.CompilerParams(vmem_limit_bytes=32 << 20),
        name="feedback_round",
    )(received, mask, postings)
    received = lax.all_to_all(send, "doc", 0, 0)
    expanded = pl.pallas_call(
        expand,
        out_shape=shape((chunk, width), bf16),
        in_specs=[VMEM] * 2,
        out_specs=VMEM,
        compiler_params=pltpu.CompilerParams(vmem_limit_bytes=32 << 20),
        name="expand",
    )(received, query)
    gathered = lax.all_to_all(jnp.broadcast_to(expanded[None], (blocks, chunk, width)), "doc", 0, 0)
    partial = dot_nt(gathered.reshape(queries, width), postings).astype(bf16)
    partial = lax.all_to_all(partial.reshape(groups, group, docs), "term", 0, 0)
    return first, jnp.sum(partial.astype(f32), axis=0)


def solution(mesh):
    return jax.shard_map(
        per_device,
        mesh=mesh,
        in_specs=(P("doc", "term"), P(), P(), P()),
        out_specs=(P("term", "doc"), P("term", "doc")),
        check_vma=False,
    )
```

```python
import jax
import jax.numpy as jnp
from jax import lax
from jax.experimental import pallas as pl
from jax.experimental.pallas import tpu as pltpu
from jax.sharding import PartitionSpec as P

expansion_weight = 0.25
lanes = 128
half = 1024
f32 = jnp.float32
bf16 = jnp.bfloat16
VMEM = pl.BlockSpec(memory_space=pltpu.VMEM)


def dot_nt(a, b):
    return lax.dot_general(a, b, (((1,), (1,)), ((), ())), preferred_element_type=f32)


def iota(shape, axis):
    return lax.broadcasted_iota(jnp.int32, shape, axis)


def first_round(terms_hbm, levels_hbm, ids_hbm, postings_hbm, send_ref, mask_ref, query_ref,
                terms_ref, levels_ref, ids_ref, postings_ref, sems):
    copies = [
        pltpu.make_async_copy(source, target, sems.at[i])
        for i, (source, target) in enumerate(
            ((terms_hbm, terms_ref), (levels_hbm, levels_ref), (ids_hbm, ids_ref), (postings_hbm, postings_ref))
        )
    ]
    for copy in copies:
        copy.start()
    copies[0].wait()
    copies[1].wait()
    slots, queries = terms_ref.shape
    docs, width = postings_ref.shape
    tiles = width // lanes
    spread = 8 * slots
    local = terms_ref[...] - lax.axis_index("term") * width
    tile_of = lax.shift_right_arithmetic(local, 7)
    lane_of = local & 127
    repeat = (iota((slots, spread), 0) == (iota((slots, spread), 1) & (slots - 1))).astype(f32).astype(bf16)
    stacked = jnp.concatenate([tile_of, lane_of, levels_ref[...]], axis=1).astype(f32).astype(bf16)
    wide = lax.dot_general(stacked, repeat, (((0,), (0,)), ((), ())), preferred_element_type=f32)
    own = lax.shift_right_logical(iota((8, spread), 1), 5) == iota((8, spread), 0)
    lane_ids = iota((lanes, spread), 0).astype(f32)
    for block in range(queries // 8):
        rows = slice(8 * block, 8 * block + 8)
        tile_now = wide[rows]
        lane_now = wide[queries + 8 * block : queries + 8 * block + 8]
        level_now = wide[2 * queries + 8 * block : 2 * queries + 8 * block + 8]
        lane_row = jnp.sum(jnp.where(own, lane_now, 0.0), axis=0, keepdims=True)
        level_own = jnp.where(own, level_now, 0.0)
        hot = jnp.where(lane_ids == lane_row, 1.0, 0.0).astype(bf16)
        parts = [jnp.where(tile_now == float(t), level_own, 0.0) for t in range(tiles)]
        totals = dot_nt(jnp.concatenate(parts, axis=0).astype(bf16), hot)
        for t in range(tiles):
            query_ref[rows, t * lanes : (t + 1) * lanes] = totals[8 * t : 8 * t + 8] * f32(0.01)
    copies[2].wait()
    place = iota((docs, queries), 0) + lax.axis_index("doc") * docs
    member = ids_ref[0:1, :] == place
    for j in range(1, ids_ref.shape[0]):
        member = member | (ids_ref[j : j + 1, :] == place)
    member = jnp.where(member, 1.0, 0.0).astype(bf16)
    wanted = iota((3 * queries, queries), 0)
    doubled = lax.shift_right_logical(wanted - queries, 3) * 4 + (wanted & 3)
    source = jnp.where(wanted < queries, wanted, doubled)
    pick = jnp.where(source == iota((3 * queries, queries), 1), 1.0, 0.0).astype(bf16)
    masks = dot_nt(pick, member)
    mask = masks[:queries]
    mask_ref[...] = masks[queries:].astype(bf16)
    copies[3].wait()
    scores = dot_nt(query_ref[...].astype(bf16), postings_ref[...])
    chosen = jnp.sum(scores * mask, axis=0, keepdims=True)
    high = chosen.astype(bf16).astype(f32)
    low = chosen - high
    steps = docs // lanes
    pieces = [x[:, i * lanes : (i + 1) * lanes] for x in (high, low) for i in range(steps)]
    tail = jnp.concatenate(pieces, axis=0).astype(bf16)
    for g in range(queries // 8):
        send_ref[g, :, 0:docs] = scores[8 * g : 8 * g + 8].astype(bf16)
        send_ref[g, :, docs : docs + lanes] = tail


def feedback_round(received_ref, mask_ref, postings_ref, first_ref, send_ref):
    groups = received_ref.shape[0]
    docs, width = postings_ref.shape
    total = received_ref[0].astype(f32)
    for g in range(1, groups):
        total = total + received_ref[g].astype(f32)
    first_ref[...] = total[:, 0:docs]
    steps = docs // lanes
    tail = total[:, docs : docs + lanes]
    weight = jnp.concatenate([tail[i : i + 1] + tail[steps + i : steps + i + 1] for i in range(steps)], axis=1)
    weight = weight.astype(bf16).astype(f32)
    mixing = (mask_ref[...].astype(f32) * weight).astype(bf16)
    postings = postings_ref[...]
    left = jnp.dot(mixing, postings[:, 0:half], preferred_element_type=f32)
    right = jnp.dot(mixing, postings[:, half:width], preferred_element_type=f32)
    sums = jnp.dot(mixing, jnp.ones((docs, lanes), bf16), preferred_element_type=f32)
    high = sums.astype(bf16).astype(f32)
    lane = iota(sums.shape, 1)
    sums = jnp.where(lane == 0, high, jnp.where(lane == 1, sums - high, 0.0))
    right = jnp.concatenate([right, sums], axis=1)
    upper = iota((8, half), 0) < 4
    for c in range(send_ref.shape[0]):
        rows = slice(8 * c, 8 * c + 8)
        send_ref[c] = jnp.where(upper, left[rows], right[rows]).astype(bf16)


def expand(received_ref, query_ref, out_ref):
    chunk, width = out_ref.shape
    total = received_ref[0].astype(f32)
    for d in range(1, received_ref.shape[0]):
        total = total + received_ref[d].astype(f32)
    rest = width - half
    weight = total[chunk:, rest : rest + 1] + total[chunk:, rest + 1 : rest + 2]
    doc = lax.axis_index("doc")
    pair = query_ref[pl.ds(pl.multiple_of(lax.shift_right_logical(doc, 1) * 8, 8), 8), :]
    mine = jnp.where((doc & 1) == 0, pair[:chunk], pair[chunk:])
    left = mine[:, :half] + expansion_weight * total[:chunk] / weight
    right = mine[:, half:] + expansion_weight * total[chunk:, :rest] / weight
    out_ref[:, 0:half] = left.astype(bf16)
    out_ref[:, half:width] = right.astype(bf16)


def per_device(postings, query_terms, query_levels, feedback_ids):
    docs, width = postings.shape
    queries = query_terms.shape[0]
    groups = lax.axis_size("term")
    blocks = lax.axis_size("doc")
    group = queries // groups
    chunk = queries // blocks
    shape = jax.ShapeDtypeStruct
    send, mask, query = pl.pallas_call(
        first_round,
        out_shape=(
            shape((groups, group, docs + lanes), bf16),
            shape((2 * queries, docs), bf16),
            shape((queries, width), f32),
        ),
        in_specs=[pl.BlockSpec(memory_space=pltpu.HBM)] * 4,
        out_specs=(VMEM, VMEM, VMEM),
        scratch_shapes=[
            pltpu.VMEM(query_terms.shape[::-1], jnp.int32),
            pltpu.VMEM(query_levels.shape[::-1], jnp.int32),
            pltpu.VMEM(feedback_ids.shape[::-1], jnp.int32),
            pltpu.VMEM((docs, width), bf16),
            pltpu.SemaphoreType.DMA((4,)),
        ],
        compiler_params=pltpu.CompilerParams(vmem_limit_bytes=32 << 20),
        name="first_round",
    )(*(
        pltpu.with_memory_space_constraint(x, pltpu.HBM)
        for x in (query_terms.T, query_levels.T, feedback_ids.T, postings)
    ))
    received = lax.all_to_all(send, "term", 0, 0)
    first, send = pl.pallas_call(
        feedback_round,
        out_shape=(shape((group, docs), f32), shape((blocks, 8, half), bf16)),
        in_specs=[VMEM] * 3,
        out_specs=(VMEM, VMEM),
        compiler_params=pltpu.CompilerParams(vmem_limit_bytes=32 << 20),
        name="feedback_round",
    )(received, mask, postings)
    received = lax.all_to_all(send, "doc", 0, 0)
    expanded = pl.pallas_call(
        expand,
        out_shape=shape((chunk, width), bf16),
        in_specs=[VMEM] * 2,
        out_specs=VMEM,
        compiler_params=pltpu.CompilerParams(vmem_limit_bytes=32 << 20),
        name="expand",
    )(received, query)
    gathered = lax.all_to_all(jnp.broadcast_to(expanded[None], (blocks, chunk, width)), "doc", 0, 0)
    partial = dot_nt(gathered.reshape(queries, width), postings).astype(bf16)
    partial = lax.all_to_all(partial.reshape(groups, group, docs), "term", 0, 0)
    return first, jnp.sum(partial.astype(f32), axis=0)


def solution(mesh):
    return jax.shard_map(
        per_device,
        mesh=mesh,
        in_specs=(P("doc", "term"), P(), P(), P()),
        out_specs=(P("term", "doc"), P("term", "doc")),
        check_vma=False,
    )
```

```python
import jax
import jax.numpy as jnp
from jax import lax
from jax.experimental import pallas as pl
from jax.experimental.pallas import tpu as pltpu
from jax.sharding import PartitionSpec as P

expansion_weight = 0.25
lanes = 128
f32 = jnp.float32
bf16 = jnp.bfloat16
VMEM = pl.BlockSpec(memory_space=pltpu.VMEM)


def dot_nt(a, b):
    return lax.dot_general(a, b, (((1,), (1,)), ((), ())), preferred_element_type=f32)


def iota(shape, axis):
    return lax.broadcasted_iota(jnp.int32, shape, axis)


def first_round(terms_hbm, levels_hbm, ids_hbm, postings_hbm, send_ref, mask_ref, query_ref, postings_ref,
                terms_ref, levels_ref, ids_ref, sems):
    pairs = [(terms_hbm, terms_ref), (levels_hbm, levels_ref), (ids_hbm, ids_ref)]
    pairs.append((postings_hbm, postings_ref))
    copies = [pltpu.make_async_copy(source, target, sems.at[i]) for i, (source, target) in enumerate(pairs)]
    for copy in copies:
        copy.start()
    copies[0].wait()
    copies[1].wait()
    slots, queries = terms_ref.shape
    docs, width = postings_ref.shape
    tiles = width // lanes
    spread = 8 * slots
    local = terms_ref[...] - lax.axis_index("term") * width
    tile_of = lax.shift_right_arithmetic(local, 7)
    lane_of = local & 127
    repeat = (iota((slots, spread), 0) == (iota((slots, spread), 1) & (slots - 1))).astype(f32).astype(bf16)
    stacked = jnp.concatenate([tile_of, lane_of, levels_ref[...]], axis=1).astype(f32).astype(bf16)
    wide = lax.dot_general(stacked, repeat, (((0,), (0,)), ((), ())), preferred_element_type=f32)
    own = lax.shift_right_logical(iota((8, spread), 1), 5) == iota((8, spread), 0)
    lane_ids = iota((lanes, spread), 0).astype(f32)
    for block in range(queries // 8):
        rows = slice(8 * block, 8 * block + 8)
        tile_now = wide[rows]
        lane_now = wide[queries + 8 * block : queries + 8 * block + 8]
        level_now = wide[2 * queries + 8 * block : 2 * queries + 8 * block + 8]
        lane_row = jnp.sum(jnp.where(own, lane_now, 0.0), axis=0, keepdims=True)
        level_own = jnp.where(own, level_now, 0.0)
        hot = jnp.where(lane_ids == lane_row, 1.0, 0.0).astype(bf16)
        parts = [jnp.where(tile_now == float(t), level_own, 0.0) for t in range(tiles)]
        totals = dot_nt(jnp.concatenate(parts, axis=0).astype(bf16), hot)
        for t in range(tiles):
            query_ref[rows, t * lanes : (t + 1) * lanes] = totals[8 * t : 8 * t + 8] * f32(0.01)
    copies[2].wait()
    place = iota((docs, queries), 0) + lax.axis_index("doc") * docs
    member = ids_ref[0:1, :] == place
    for j in range(1, ids_ref.shape[0]):
        member = member | (ids_ref[j : j + 1, :] == place)
    member = jnp.where(member, 1.0, 0.0).astype(bf16)
    same = jnp.where(iota((queries, queries), 0) == iota((queries, queries), 1), 1.0, 0.0).astype(bf16)
    mask = dot_nt(same, member)
    mask_ref[...] = mask.astype(bf16)
    copies[3].wait()
    scores = dot_nt(query_ref[...].astype(bf16), postings_ref[...])
    chosen = jnp.sum(scores * mask, axis=0, keepdims=True)
    tail = jnp.concatenate([chosen[:, i : i + lanes] for i in range(0, docs, lanes)], axis=0).astype(bf16)
    for g in range(queries // 8):
        send_ref[g, :, 0:docs] = scores[8 * g : 8 * g + 4].astype(bf16)
        send_ref[g, :, docs : 2 * docs] = scores[8 * g + 4 : 8 * g + 8].astype(bf16)
        send_ref[g, :, 2 * docs :] = tail


def feedback_round(received_ref, mask_ref, postings_ref, first_ref, send_ref):
    groups = received_ref.shape[0]
    docs, width = postings_ref.shape
    total = received_ref[0].astype(f32)
    for g in range(1, groups):
        total = total + received_ref[g].astype(f32)
    first_ref[0:4] = total[:, 0:docs]
    first_ref[4:8] = total[:, docs : 2 * docs]
    tail = total[:, 2 * docs :]
    weight = jnp.concatenate([tail[i : i + 1] for i in range(docs // lanes)], axis=1)
    weight = weight.astype(bf16).astype(f32)
    mixing = (mask_ref[...].astype(f32) * weight).astype(bf16)
    postings = postings_ref[...]
    numerator = jnp.dot(mixing, postings, preferred_element_type=f32)
    sums = jnp.dot(mixing, jnp.ones((docs, lanes), bf16), preferred_element_type=f32)
    high = sums.astype(bf16).astype(f32)
    lane = iota(sums.shape, 1)
    sums = jnp.where(lane == 0, high, jnp.where(lane == 1, sums - high, 0.0))
    for c in range(send_ref.shape[0]):
        rows = slice(4 * c, 4 * c + 4)
        send_ref[c, :, 0:width] = numerator[rows].astype(bf16)
        send_ref[c, :, width : width + lanes] = sums[rows].astype(bf16)


def expand(received_ref, query_ref, out_ref):
    chunk, width = out_ref.shape
    total = received_ref[0].astype(f32)
    for d in range(1, received_ref.shape[0]):
        total = total + received_ref[d].astype(f32)
    weight = total[:, width : width + 1] + total[:, width + 1 : width + 2]
    doc = lax.axis_index("doc")
    pair = query_ref[pl.ds(pl.multiple_of(lax.shift_right_logical(doc, 1) * 8, 8), 8), :]
    mine = jnp.where((doc & 1) == 0, pair[:chunk], pair[chunk:])
    out_ref[...] = (mine + expansion_weight * total[:, :width] / weight).astype(bf16)


def per_device(postings, query_terms, query_levels, feedback_ids):
    docs, width = postings.shape
    queries = query_terms.shape[0]
    groups = lax.axis_size("term")
    blocks = lax.axis_size("doc")
    group = queries // groups
    chunk = queries // blocks
    shape = jax.ShapeDtypeStruct
    send, mask, query, postings = pl.pallas_call(
        first_round,
        out_shape=(
            shape((groups, group // 2, 2 * docs + lanes), bf16),
            shape((queries, docs), bf16),
            shape((queries, width), f32),
            shape((docs, width), bf16),
        ),
        in_specs=[pl.BlockSpec(memory_space=pltpu.HBM)] * 4,
        out_specs=(VMEM,) * 4,
        scratch_shapes=[
            pltpu.VMEM(query_terms.shape[::-1], jnp.int32),
            pltpu.VMEM(query_levels.shape[::-1], jnp.int32),
            pltpu.VMEM(feedback_ids.shape[::-1], jnp.int32),
            pltpu.SemaphoreType.DMA((4,)),
        ],
        compiler_params=pltpu.CompilerParams(vmem_limit_bytes=32 << 20),
        name="first_round",
    )(*(
        pltpu.with_memory_space_constraint(x, pltpu.HBM)
        for x in (query_terms.T, query_levels.T, feedback_ids.T, postings)
    ))
    received = lax.all_to_all(send, "term", 0, 0)
    first, send = pl.pallas_call(
        feedback_round,
        out_shape=(shape((group, docs), f32), shape((blocks, chunk, width + lanes), bf16)),
        in_specs=[VMEM] * 3,
        out_specs=(VMEM, VMEM),
        compiler_params=pltpu.CompilerParams(vmem_limit_bytes=32 << 20),
        name="feedback_round",
    )(received, mask, postings)
    received = lax.all_to_all(send, "doc", 0, 0)
    expanded = pl.pallas_call(
        expand,
        out_shape=shape((chunk, width), bf16),
        in_specs=[VMEM] * 2,
        out_specs=VMEM,
        compiler_params=pltpu.CompilerParams(vmem_limit_bytes=32 << 20),
        name="expand",
    )(received, query)
    gathered = lax.all_to_all(jnp.broadcast_to(expanded[None], (blocks, chunk, width)), "doc", 0, 0)
    partial = dot_nt(gathered.reshape(queries, width), postings).astype(bf16)
    partial = lax.all_to_all(partial.reshape(groups, group, docs), "term", 0, 0)
    return first, jnp.sum(partial.astype(f32), axis=0)


def solution(mesh):
    return jax.shard_map(
        per_device,
        mesh=mesh,
        in_specs=(P("doc", "term"), P(), P(), P()),
        out_specs=(P("term", "doc"), P("term", "doc")),
        check_vma=False,
    )
```

```python
import functools

import jax
import jax.numpy as jnp
from jax import lax
from jax.experimental import pallas as pl
from jax.experimental.pallas import tpu as pltpu
from jax.sharding import PartitionSpec as P

expansion_weight = 0.25
lanes = 128
first_top = 32 * 2.55 * 3.0 * 1.001
f32 = jnp.float32
bf16 = jnp.bfloat16
VMEM = pl.BlockSpec(memory_space=pltpu.VMEM)


def dot_nt(a, b):
    return lax.dot_general(a, b, (((1,), (1,)), ((), ())), preferred_element_type=f32)


def iota(shape, axis):
    return lax.broadcasted_iota(jnp.int32, shape, axis)


def encode(x, top):
    root = jnp.sqrt(jnp.sqrt(jnp.sqrt(x * f32(1.0 / top))))
    return (jnp.round(root * f32(65535.0)).astype(jnp.int32) - 32768).astype(jnp.int16)


def decode(codes, top):
    root = (codes.astype(jnp.int32).astype(f32) + f32(32768.0)) * f32(top**0.125 / 65535.0)
    square = root * root
    fourth = square * square
    return fourth * fourth


def first_round(terms_hbm, levels_hbm, ids_hbm, postings_hbm, send_ref, mask_ref, query_ref, postings_ref,
                terms_ref, levels_ref, ids_ref, sems):
    pairs = [(terms_hbm, terms_ref), (levels_hbm, levels_ref), (ids_hbm, ids_ref)]
    pairs.append((postings_hbm, postings_ref))
    copies = [pltpu.make_async_copy(source, target, sems.at[i]) for i, (source, target) in enumerate(pairs)]
    for copy in copies:
        copy.start()
    copies[0].wait()
    copies[1].wait()
    slots, queries = terms_ref.shape
    docs, width = postings_ref.shape
    tiles = width // lanes
    spread = 8 * slots
    local = terms_ref[...] - lax.axis_index("term") * width
    tile_of = lax.shift_right_arithmetic(local, 7)
    lane_of = local & 127
    repeat = (iota((slots, spread), 0) == (iota((slots, spread), 1) & (slots - 1))).astype(f32).astype(bf16)
    stacked = jnp.concatenate([tile_of, lane_of, levels_ref[...]], axis=1).astype(f32).astype(bf16)
    wide = lax.dot_general(stacked, repeat, (((0,), (0,)), ((), ())), preferred_element_type=f32)
    own = lax.shift_right_logical(iota((8, spread), 1), 5) == iota((8, spread), 0)
    lane_ids = iota((lanes, spread), 0).astype(f32)
    for block in range(queries // 8):
        rows = slice(8 * block, 8 * block + 8)
        tile_now = wide[rows]
        lane_now = wide[queries + 8 * block : queries + 8 * block + 8]
        level_now = wide[2 * queries + 8 * block : 2 * queries + 8 * block + 8]
        lane_row = jnp.sum(jnp.where(own, lane_now, 0.0), axis=0, keepdims=True)
        level_own = jnp.where(own, level_now, 0.0)
        hot = jnp.where(lane_ids == lane_row, 1.0, 0.0).astype(bf16)
        parts = [jnp.where(tile_now == float(t), level_own, 0.0) for t in range(tiles)]
        totals = dot_nt(jnp.concatenate(parts, axis=0).astype(bf16), hot)
        for t in range(tiles):
            query_ref[rows, t * lanes : (t + 1) * lanes] = totals[8 * t : 8 * t + 8] * f32(0.01)
    copies[2].wait()
    place = iota((docs, queries), 0) + lax.axis_index("doc") * docs
    member = ids_ref[0:1, :] == place
    for j in range(1, ids_ref.shape[0]):
        member = member | (ids_ref[j : j + 1, :] == place)
    member = jnp.where(member, 1.0, 0.0).astype(bf16)
    same = jnp.where(iota((queries, queries), 0) == iota((queries, queries), 1), 1.0, 0.0).astype(bf16)
    mask = dot_nt(same, member)
    mask_ref[...] = mask.astype(bf16)
    copies[3].wait()
    scores = dot_nt(query_ref[...].astype(bf16), postings_ref[...])
    chosen = jnp.sum(scores * mask, axis=0, keepdims=True)
    tail = jnp.concatenate([chosen[:, i : i + lanes] for i in range(0, docs, lanes)], axis=0)
    tail = encode(tail, first_top)
    codes = encode(scores, first_top)
    for g in range(queries // 8):
        send_ref[g, :, 0:docs] = codes[8 * g : 8 * g + 4]
        send_ref[g, :, docs : 2 * docs] = codes[8 * g + 4 : 8 * g + 8]
        send_ref[g, :, 2 * docs :] = tail


def feedback_round(received_ref, mask_ref, postings_ref, send_ref):
    groups = received_ref.shape[0]
    docs, width = postings_ref.shape
    tail = decode(received_ref[0, :, 2 * docs :], first_top)
    for g in range(1, groups):
        tail = tail + decode(received_ref[g, :, 2 * docs :], first_top)
    weight = jnp.concatenate([tail[i : i + 1] for i in range(docs // lanes)], axis=1)
    weight = weight.astype(bf16).astype(f32)
    mixing = (mask_ref[...].astype(f32) * weight).astype(bf16)
    postings = postings_ref[...]
    numerator = jnp.dot(mixing, postings, preferred_element_type=f32)
    sums = jnp.dot(mixing, jnp.ones((docs, lanes), bf16), preferred_element_type=f32)
    high = sums.astype(bf16).astype(f32)
    lane = iota(sums.shape, 1)
    sums = jnp.where(lane == 0, high, jnp.where(lane == 1, sums - high, 0.0))
    for c in range(send_ref.shape[0]):
        rows = slice(4 * c, 4 * c + 4)
        send_ref[c, :, 0:width] = numerator[rows].astype(bf16)
        send_ref[c, :, width : width + lanes] = sums[rows].astype(bf16)


def totals(first_codes_ref, final_codes_ref, first_ref, final_ref, *, final_top):
    groups, rows, docs = final_codes_ref.shape
    folded = rows // 2
    for side in range(2):
        columns = slice(side * docs, (side + 1) * docs)
        total = decode(first_codes_ref[0, :, columns], first_top)
        for g in range(1, groups):
            total = total + decode(first_codes_ref[g, :, columns], first_top)
        first_ref[side * folded : (side + 1) * folded] = total
    total = decode(final_codes_ref[0], final_top)
    for g in range(1, groups):
        total = total + decode(final_codes_ref[g], final_top)
    final_ref[...] = total


def expand(received_ref, query_ref, out_ref):
    chunk, width = out_ref.shape
    total = received_ref[0].astype(f32)
    for d in range(1, received_ref.shape[0]):
        total = total + received_ref[d].astype(f32)
    weight = total[:, width : width + 1] + total[:, width + 1 : width + 2]
    doc = lax.axis_index("doc")
    pair = query_ref[pl.ds(pl.multiple_of(lax.shift_right_logical(doc, 1) * 8, 8), 8), :]
    mine = jnp.where((doc & 1) == 0, pair[:chunk], pair[chunk:])
    out_ref[...] = (mine + expansion_weight * total[:, :width] / weight).astype(bf16)


def per_device(postings, query_terms, query_levels, feedback_ids):
    docs, width = postings.shape
    queries = query_terms.shape[0]
    groups = lax.axis_size("term")
    blocks = lax.axis_size("doc")
    group = queries // groups
    chunk = queries // blocks
    shape = jax.ShapeDtypeStruct
    final_top = first_top + expansion_weight * 3.0 * 3.0 * 1.01 * width
    send, mask, query, postings = pl.pallas_call(
        first_round,
        out_shape=(
            shape((groups, group // 2, 2 * docs + lanes), jnp.int16),
            shape((queries, docs), bf16),
            shape((queries, width), f32),
            shape((docs, width), bf16),
        ),
        in_specs=[pl.BlockSpec(memory_space=pltpu.HBM)] * 4,
        out_specs=(VMEM,) * 4,
        scratch_shapes=[
            pltpu.VMEM(query_terms.shape[::-1], jnp.int32),
            pltpu.VMEM(query_levels.shape[::-1], jnp.int32),
            pltpu.VMEM(feedback_ids.shape[::-1], jnp.int32),
            pltpu.SemaphoreType.DMA((4,)),
        ],
        compiler_params=pltpu.CompilerParams(vmem_limit_bytes=32 << 20),
        name="first_round",
    )(*(
        pltpu.with_memory_space_constraint(x, pltpu.HBM)
        for x in (query_terms.T, query_levels.T, feedback_ids.T, postings)
    ))
    first_codes = lax.all_to_all(send, "term", 0, 0)
    send = pl.pallas_call(
        feedback_round,
        out_shape=shape((blocks, chunk, width + lanes), bf16),
        in_specs=[VMEM] * 3,
        out_specs=VMEM,
        compiler_params=pltpu.CompilerParams(vmem_limit_bytes=32 << 20),
        name="feedback_round",
    )(first_codes, mask, postings)
    received = lax.all_to_all(send, "doc", 0, 0)
    expanded = pl.pallas_call(
        expand,
        out_shape=shape((chunk, width), bf16),
        in_specs=[VMEM] * 2,
        out_specs=VMEM,
        compiler_params=pltpu.CompilerParams(vmem_limit_bytes=32 << 20),
        name="expand",
    )(received, query)
    gathered = lax.all_to_all(jnp.broadcast_to(expanded[None], (blocks, chunk, width)), "doc", 0, 0)
    partial = encode(dot_nt(gathered.reshape(queries, width), postings), final_top)
    partial = lax.all_to_all(partial.reshape(groups, group, docs), "term", 0, 0)
    return pl.pallas_call(
        functools.partial(totals, final_top=final_top),
        out_shape=(shape((group, docs), f32),) * 2,
        in_specs=[VMEM] * 2,
        out_specs=(VMEM,) * 2,
        compiler_params=pltpu.CompilerParams(vmem_limit_bytes=32 << 20),
        name="totals",
    )(first_codes, partial)


def solution(mesh):
    return jax.shard_map(
        per_device,
        mesh=mesh,
        in_specs=(P("doc", "term"), P(), P(), P()),
        out_specs=(P("term", "doc"), P("term", "doc")),
        check_vma=False,
    )
```

```python
import functools

import jax
import jax.numpy as jnp
from jax import lax
from jax.experimental import pallas as pl
from jax.experimental.pallas import tpu as pltpu
from jax.sharding import PartitionSpec as P

expansion_weight = 0.25
lanes = 128
first_top = 32 * 2.55 * 3.0 * 1.001
f32 = jnp.float32
bf16 = jnp.bfloat16
VMEM = pl.BlockSpec(memory_space=pltpu.VMEM)


def dot_nt(a, b):
    return lax.dot_general(a, b, (((1,), (1,)), ((), ())), preferred_element_type=f32)


def iota(shape, axis):
    return lax.broadcasted_iota(jnp.int32, shape, axis)


def encode(x, top):
    root = jnp.maximum(x * f32(1.0 / top), f32(1e-37))
    for _ in range(3):
        root = root * lax.rsqrt(root)
    return ((root * f32(65535.0) + f32(0.5)).astype(jnp.int32) - 32768).astype(jnp.int16)


def decode(codes, top):
    root = (codes.astype(jnp.int32).astype(f32) + f32(32768.0)) * f32(top**0.125 / 65535.0)
    square = root * root
    fourth = square * square
    return fourth * fourth


def first_round(terms_hbm, levels_hbm, ids_hbm, postings_hbm, send_ref, mask_ref, query_ref, postings_ref,
                terms_ref, levels_ref, ids_ref, sems):
    pairs = [(terms_hbm, terms_ref), (levels_hbm, levels_ref), (ids_hbm, ids_ref)]
    pairs.append((postings_hbm, postings_ref))
    copies = [pltpu.make_async_copy(source, target, sems.at[i]) for i, (source, target) in enumerate(pairs)]
    for copy in copies:
        copy.start()
    copies[0].wait()
    copies[1].wait()
    slots, queries = terms_ref.shape
    docs, width = postings_ref.shape
    tiles = width // lanes
    spread = 8 * slots
    local = terms_ref[...] - lax.axis_index("term") * width
    tile_of = lax.shift_right_arithmetic(local, 7)
    lane_of = local & 127
    repeat = (iota((slots, spread), 0) == (iota((slots, spread), 1) & (slots - 1))).astype(f32).astype(bf16)
    stacked = jnp.concatenate([tile_of, lane_of, levels_ref[...]], axis=1).astype(f32).astype(bf16)
    wide = lax.dot_general(stacked, repeat, (((0,), (0,)), ((), ())), preferred_element_type=f32)
    own = lax.shift_right_logical(iota((8, spread), 1), 5) == iota((8, spread), 0)
    lane_ids = iota((lanes, spread), 0).astype(f32)
    for block in range(queries // 8):
        rows = slice(8 * block, 8 * block + 8)
        tile_now = wide[rows]
        lane_now = wide[queries + 8 * block : queries + 8 * block + 8]
        level_now = wide[2 * queries + 8 * block : 2 * queries + 8 * block + 8]
        lane_row = jnp.sum(jnp.where(own, lane_now, 0.0), axis=0, keepdims=True)
        level_own = jnp.where(own, level_now, 0.0)
        hot = jnp.where(lane_ids == lane_row, 1.0, 0.0).astype(bf16)
        parts = [jnp.where(tile_now == float(t), level_own, 0.0) for t in range(tiles)]
        totals = dot_nt(jnp.concatenate(parts, axis=0).astype(bf16), hot)
        for t in range(tiles):
            query_ref[rows, t * lanes : (t + 1) * lanes] = totals[8 * t : 8 * t + 8] * f32(0.01)
    copies[2].wait()
    place = (iota((docs, queries), 0) + lax.axis_index("doc") * docs).astype(jnp.int16)
    ids = ids_ref[...].astype(jnp.int16)
    member = ids[0:1, :] == place
    for j in range(1, ids.shape[0]):
        member = member | (ids[j : j + 1, :] == place)
    member = jnp.where(member, jnp.ones((), bf16), jnp.zeros((), bf16))
    same = jnp.where(iota((queries, queries), 0) == iota((queries, queries), 1), 1.0, 0.0).astype(bf16)
    mask = dot_nt(same, member)
    mask_ref[...] = mask.astype(bf16)
    copies[3].wait()
    scores = dot_nt(query_ref[...].astype(bf16), postings_ref[...])
    chosen = jnp.sum(scores * mask, axis=0, keepdims=True)
    tail = jnp.concatenate([chosen[:, i : i + lanes] for i in range(0, docs, lanes)], axis=0)
    tail = encode(tail, first_top)
    codes = encode(scores, first_top)
    for g in range(queries // 8):
        send_ref[g, :, 0:docs] = codes[8 * g : 8 * g + 4]
        send_ref[g, :, docs : 2 * docs] = codes[8 * g + 4 : 8 * g + 8]
        send_ref[g, :, 2 * docs :] = tail


def feedback_round(received_ref, mask_ref, postings_ref, send_ref):
    groups = received_ref.shape[0]
    docs, width = postings_ref.shape
    tail = decode(received_ref[0, :, 2 * docs :], first_top)
    for g in range(1, groups):
        tail = tail + decode(received_ref[g, :, 2 * docs :], first_top)
    weight = jnp.concatenate([tail[i : i + 1] for i in range(docs // lanes)], axis=1)
    weight = weight.astype(bf16).astype(f32)
    mixing = (mask_ref[...].astype(f32) * weight).astype(bf16)
    postings = postings_ref[...]
    numerator = jnp.dot(mixing, postings, preferred_element_type=f32)
    sums = jnp.dot(mixing, jnp.ones((docs, lanes), bf16), preferred_element_type=f32)
    high = sums.astype(bf16).astype(f32)
    lane = iota(sums.shape, 1)
    sums = jnp.where(lane == 0, high, jnp.where(lane == 1, sums - high, 0.0))
    for c in range(send_ref.shape[0]):
        rows = slice(4 * c, 4 * c + 4)
        send_ref[c, :, 0:width] = numerator[rows].astype(bf16)
        send_ref[c, :, width : width + lanes] = sums[rows].astype(bf16)


def totals(first_codes_ref, final_codes_ref, first_ref, final_ref, *, final_top):
    groups, rows, docs = final_codes_ref.shape
    folded = rows // 2
    for side in range(2):
        columns = slice(side * docs, (side + 1) * docs)
        total = decode(first_codes_ref[0, :, columns], first_top)
        for g in range(1, groups):
            total = total + decode(first_codes_ref[g, :, columns], first_top)
        first_ref[side * folded : (side + 1) * folded] = total
    total = decode(final_codes_ref[0], final_top)
    for g in range(1, groups):
        total = total + decode(final_codes_ref[g], final_top)
    final_ref[...] = total


def expand(received_ref, query_ref, out_ref):
    chunk, width = out_ref.shape
    total = received_ref[0].astype(f32)
    for d in range(1, received_ref.shape[0]):
        total = total + received_ref[d].astype(f32)
    weight = total[:, width : width + 1] + total[:, width + 1 : width + 2]
    doc = lax.axis_index("doc")
    pair = query_ref[pl.ds(pl.multiple_of(lax.shift_right_logical(doc, 1) * 8, 8), 8), :]
    mine = jnp.where((doc & 1) == 0, pair[:chunk], pair[chunk:])
    out_ref[...] = (mine + expansion_weight * total[:, :width] / weight).astype(bf16)


def per_device(postings, query_terms, query_levels, feedback_ids):
    docs, width = postings.shape
    queries = query_terms.shape[0]
    groups = lax.axis_size("term")
    blocks = lax.axis_size("doc")
    group = queries // groups
    chunk = queries // blocks
    shape = jax.ShapeDtypeStruct
    final_top = first_top + expansion_weight * 3.0 * 3.0 * 1.01 * width
    send, mask, query, postings = pl.pallas_call(
        first_round,
        out_shape=(
            shape((groups, group // 2, 2 * docs + lanes), jnp.int16),
            shape((queries, docs), bf16),
            shape((queries, width), f32),
            shape((docs, width), bf16),
        ),
        in_specs=[pl.BlockSpec(memory_space=pltpu.HBM)] * 4,
        out_specs=(VMEM,) * 4,
        scratch_shapes=[
            pltpu.VMEM(query_terms.shape[::-1], jnp.int32),
            pltpu.VMEM(query_levels.shape[::-1], jnp.int32),
            pltpu.VMEM(feedback_ids.shape[::-1], jnp.int32),
            pltpu.SemaphoreType.DMA((4,)),
        ],
        compiler_params=pltpu.CompilerParams(vmem_limit_bytes=32 << 20),
        name="first_round",
    )(*(
        pltpu.with_memory_space_constraint(x, pltpu.HBM)
        for x in (query_terms.T, query_levels.T, feedback_ids.T, postings)
    ))
    first_codes = lax.all_to_all(send, "term", 0, 0)
    send = pl.pallas_call(
        feedback_round,
        out_shape=shape((blocks, chunk, width + lanes), bf16),
        in_specs=[VMEM] * 3,
        out_specs=VMEM,
        compiler_params=pltpu.CompilerParams(vmem_limit_bytes=32 << 20),
        name="feedback_round",
    )(first_codes, mask, postings)
    received = lax.all_to_all(send, "doc", 0, 0)
    expanded = pl.pallas_call(
        expand,
        out_shape=shape((chunk, width), bf16),
        in_specs=[VMEM] * 2,
        out_specs=VMEM,
        compiler_params=pltpu.CompilerParams(vmem_limit_bytes=32 << 20),
        name="expand",
    )(received, query)
    gathered = lax.all_to_all(jnp.broadcast_to(expanded[None], (blocks, chunk, width)), "doc", 0, 0)
    partial = encode(dot_nt(gathered.reshape(queries, width), postings), final_top)
    partial = lax.all_to_all(partial.reshape(groups, group, docs), "term", 0, 0)
    return pl.pallas_call(
        functools.partial(totals, final_top=final_top),
        out_shape=(shape((group, docs), f32),) * 2,
        in_specs=[VMEM] * 2,
        out_specs=(VMEM,) * 2,
        compiler_params=pltpu.CompilerParams(vmem_limit_bytes=32 << 20),
        name="totals",
    )(first_codes, partial)


def solution(mesh):
    return jax.shard_map(
        per_device,
        mesh=mesh,
        in_specs=(P("doc", "term"), P(), P(), P()),
        out_specs=(P("term", "doc"), P("term", "doc")),
        check_vma=False,
    )
```

```python
import functools

import jax
import jax.numpy as jnp
from jax import lax
from jax.experimental import pallas as pl
from jax.experimental.pallas import tpu as pltpu
from jax.sharding import PartitionSpec as P

expansion_weight = 0.25
lanes = 128
first_top = 32 * 2.55 * 3.0 * 1.001
f32 = jnp.float32
bf16 = jnp.bfloat16
VMEM = pl.BlockSpec(memory_space=pltpu.VMEM)


def dot_nt(a, b):
    return lax.dot_general(a, b, (((1,), (1,)), ((), ())), preferred_element_type=f32)


def iota(shape, axis):
    return lax.broadcasted_iota(jnp.int32, shape, axis)


def encode(x, top):
    root = jnp.maximum(x * f32(1.0 / top), f32(1e-37))
    for _ in range(3):
        root = root * lax.rsqrt(root)
    return ((root * f32(65535.0) + f32(0.5)).astype(jnp.int32) - 32768).astype(jnp.int16)


def decode(codes, top):
    root = (codes.astype(jnp.int32).astype(f32) + f32(32768.0)) * f32(top**0.125 / 65535.0)
    square = root * root
    fourth = square * square
    return fourth * fourth


def first_round(terms_hbm, levels_hbm, ids_hbm, postings_hbm, send_ref, mask_ref, query_ref, postings_ref,
                terms_ref, levels_ref, ids_ref, sems):
    pairs = [(terms_hbm, terms_ref), (levels_hbm, levels_ref), (ids_hbm, ids_ref)]
    pairs.append((postings_hbm, postings_ref))
    copies = [pltpu.make_async_copy(source, target, sems.at[i]) for i, (source, target) in enumerate(pairs)]
    for copy in copies:
        copy.start()
    copies[0].wait()
    copies[1].wait()
    slots, queries = terms_ref.shape
    docs, width = postings_ref.shape
    tiles = width // lanes
    spread = 8 * slots
    local = terms_ref[...] - lax.axis_index("term") * width
    tile_of = lax.shift_right_arithmetic(local, 7)
    lane_of = local & 127
    repeat = (iota((slots, spread), 0) == (iota((slots, spread), 1) & (slots - 1))).astype(f32).astype(bf16)
    stacked = jnp.concatenate([tile_of, lane_of, levels_ref[...]], axis=1).astype(f32).astype(bf16)
    wide = lax.dot_general(stacked, repeat, (((0,), (0,)), ((), ())), preferred_element_type=f32)
    own = lax.shift_right_logical(iota((8, spread), 1), 5) == iota((8, spread), 0)
    lane_ids = iota((lanes, spread), 0).astype(f32)
    for block in range(queries // 8):
        rows = slice(8 * block, 8 * block + 8)
        tile_now = wide[rows]
        lane_now = wide[queries + 8 * block : queries + 8 * block + 8]
        level_now = wide[2 * queries + 8 * block : 2 * queries + 8 * block + 8]
        lane_row = jnp.sum(jnp.where(own, lane_now, 0.0), axis=0, keepdims=True)
        level_own = jnp.where(own, level_now, 0.0)
        hot = jnp.where(lane_ids == lane_row, 1.0, 0.0).astype(bf16)
        parts = [jnp.where(tile_now == float(t), level_own, 0.0) for t in range(tiles)]
        totals = dot_nt(jnp.concatenate(parts, axis=0).astype(bf16), hot)
        for t in range(tiles):
            query_ref[rows, t * lanes : (t + 1) * lanes] = totals[8 * t : 8 * t + 8] * f32(0.01)
    copies[2].wait()
    place = (iota((docs, queries), 0) + lax.axis_index("doc") * docs).astype(jnp.int16)
    ids = ids_ref[...].astype(jnp.int16)
    member = ids[0:1, :] == place
    for j in range(1, ids.shape[0]):
        member = member | (ids[j : j + 1, :] == place)
    member = jnp.where(member, jnp.ones((), bf16), jnp.zeros((), bf16))
    same = jnp.where(iota((queries, queries), 0) == iota((queries, queries), 1), 1.0, 0.0).astype(bf16)
    mask = dot_nt(same, member)
    mask_ref[...] = mask.astype(bf16)
    copies[3].wait()
    scores = dot_nt(query_ref[...].astype(bf16), postings_ref[...])
    chosen = jnp.sum(scores * mask, axis=0, keepdims=True)
    tail = jnp.concatenate([chosen[:, i : i + lanes] for i in range(0, docs, lanes)], axis=0)
    tail = encode(tail, first_top)
    codes = encode(scores, first_top)
    for g in range(queries // 8):
        send_ref[g, :, 0:docs] = codes[8 * g : 8 * g + 4]
        send_ref[g, :, docs : 2 * docs] = codes[8 * g + 4 : 8 * g + 8]
        send_ref[g, :, 2 * docs :] = tail


def feedback_round(received_ref, mask_ref, postings_ref, send_ref):
    groups = received_ref.shape[0]
    docs, width = postings_ref.shape
    tail = decode(received_ref[0, :, 2 * docs :], first_top)
    for g in range(1, groups):
        tail = tail + decode(received_ref[g, :, 2 * docs :], first_top)
    weight = jnp.concatenate([tail[i : i + 1] for i in range(docs // lanes)], axis=1)
    weight = weight.astype(bf16).astype(f32)
    mixing = (mask_ref[...].astype(f32) * weight).astype(bf16)
    postings = postings_ref[...]
    numerator = jnp.dot(mixing, postings, preferred_element_type=f32)
    sums = jnp.dot(mixing, jnp.ones((docs, lanes), bf16), preferred_element_type=f32)
    high = sums.astype(bf16).astype(f32)
    lane = iota(sums.shape, 1)
    sums = jnp.where(lane == 0, high, jnp.where(lane == 1, sums - high, 0.0))
    for c in range(send_ref.shape[0]):
        rows = slice(4 * c, 4 * c + 4)
        send_ref[c, :, 0:width] = numerator[rows].astype(bf16)
        send_ref[c, :, width : width + lanes] = sums[rows].astype(bf16)


def totals(first_codes_ref, final_codes_ref, first_ref, final_ref, *, final_top):
    groups, rows, docs = final_codes_ref.shape
    folded = rows // 2
    for side in range(2):
        columns = slice(side * docs, (side + 1) * docs)
        total = decode(first_codes_ref[0, :, columns], first_top)
        for g in range(1, groups):
            total = total + decode(first_codes_ref[g, :, columns], first_top)
        first_ref[side * folded : (side + 1) * folded] = total
    total = decode(final_codes_ref[0], final_top)
    for g in range(1, groups):
        total = total + decode(final_codes_ref[g], final_top)
    final_ref[...] = total


def expand(received_ref, query_ref, out_ref):
    blocks, chunk, width = out_ref.shape
    total = received_ref[0].astype(f32)
    for d in range(1, received_ref.shape[0]):
        total = total + received_ref[d].astype(f32)
    weight = total[:, width : width + 1] + total[:, width + 1 : width + 2]
    doc = lax.axis_index("doc")
    pair = query_ref[pl.ds(pl.multiple_of(lax.shift_right_logical(doc, 1) * 8, 8), 8), :]
    mine = jnp.where((doc & 1) == 0, pair[:chunk], pair[chunk:])
    mine = (mine + expansion_weight * total[:, :width] / weight).astype(bf16)
    for d in range(blocks):
        out_ref[d] = mine


def rescore(gathered_ref, postings_ref, send_ref, rows_ref, *, final_top):
    chunk = gathered_ref.shape[1]
    for d in range(gathered_ref.shape[0]):
        rows_ref[chunk * d : chunk * d + chunk] = gathered_ref[d]
    codes = encode(dot_nt(rows_ref[...], postings_ref[...]), final_top)
    group = send_ref.shape[1]
    for g in range(send_ref.shape[0]):
        send_ref[g] = codes[group * g : group * g + group]


def per_device(postings, query_terms, query_levels, feedback_ids):
    docs, width = postings.shape
    queries = query_terms.shape[0]
    groups = lax.axis_size("term")
    blocks = lax.axis_size("doc")
    group = queries // groups
    chunk = queries // blocks
    shape = jax.ShapeDtypeStruct
    final_top = first_top + expansion_weight * 3.0 * 3.0 * 1.01 * width
    send, mask, query, postings = pl.pallas_call(
        first_round,
        out_shape=(
            shape((groups, group // 2, 2 * docs + lanes), jnp.int16),
            shape((queries, docs), bf16),
            shape((queries, width), f32),
            shape((docs, width), bf16),
        ),
        in_specs=[pl.BlockSpec(memory_space=pltpu.HBM)] * 4,
        out_specs=(VMEM,) * 4,
        scratch_shapes=[
            pltpu.VMEM(query_terms.shape[::-1], jnp.int32),
            pltpu.VMEM(query_levels.shape[::-1], jnp.int32),
            pltpu.VMEM(feedback_ids.shape[::-1], jnp.int32),
            pltpu.SemaphoreType.DMA((4,)),
        ],
        compiler_params=pltpu.CompilerParams(vmem_limit_bytes=32 << 20),
        name="first_round",
    )(*(
        pltpu.with_memory_space_constraint(x, pltpu.HBM)
        for x in (query_terms.T, query_levels.T, feedback_ids.T, postings)
    ))
    first_codes = lax.all_to_all(send, "term", 0, 0)
    send = pl.pallas_call(
        feedback_round,
        out_shape=shape((blocks, chunk, width + lanes), bf16),
        in_specs=[VMEM] * 3,
        out_specs=VMEM,
        compiler_params=pltpu.CompilerParams(vmem_limit_bytes=32 << 20),
        name="feedback_round",
    )(first_codes, mask, postings)
    received = lax.all_to_all(send, "doc", 0, 0)
    expanded = pl.pallas_call(
        expand,
        out_shape=shape((blocks, chunk, width), bf16),
        in_specs=[VMEM] * 2,
        out_specs=VMEM,
        compiler_params=pltpu.CompilerParams(vmem_limit_bytes=32 << 20),
        name="expand",
    )(received, query)
    gathered = lax.all_to_all(expanded, "doc", 0, 0)
    send = pl.pallas_call(
        functools.partial(rescore, final_top=final_top),
        out_shape=shape((groups, group, docs), jnp.int16),
        in_specs=[VMEM] * 2,
        out_specs=VMEM,
        scratch_shapes=[pltpu.VMEM((queries, width), bf16)],
        compiler_params=pltpu.CompilerParams(vmem_limit_bytes=32 << 20),
        name="rescore",
    )(gathered, postings)
    partial = lax.all_to_all(send, "term", 0, 0)
    return pl.pallas_call(
        functools.partial(totals, final_top=final_top),
        out_shape=(shape((group, docs), f32),) * 2,
        in_specs=[VMEM] * 2,
        out_specs=(VMEM,) * 2,
        compiler_params=pltpu.CompilerParams(vmem_limit_bytes=32 << 20),
        name="totals",
    )(first_codes, partial)


def solution(mesh):
    return jax.shard_map(
        per_device,
        mesh=mesh,
        in_specs=(P("doc", "term"), P(), P(), P()),
        out_specs=(P("term", "doc"), P("term", "doc")),
        check_vma=False,
    )
```

```python
import functools

import jax
import jax.numpy as jnp
from jax import lax
from jax.experimental import pallas as pl
from jax.experimental.pallas import tpu as pltpu
from jax.sharding import PartitionSpec as P

expansion_weight = 0.25
lanes = 128
first_top = 32 * 2.55 * 3.0 * 1.001
f32 = jnp.float32
bf16 = jnp.bfloat16
VMEM = pl.BlockSpec(memory_space=pltpu.VMEM)


def dot_nt(a, b):
    return lax.dot_general(a, b, (((1,), (1,)), ((), ())), preferred_element_type=f32)


def iota(shape, axis):
    return lax.broadcasted_iota(jnp.int32, shape, axis)


def encode(x, top):
    root = jnp.maximum(x * f32(1.0 / top), f32(1e-37))
    for _ in range(3):
        root = root * lax.rsqrt(root)
    return ((root * f32(65535.0) + f32(0.5)).astype(jnp.int32) - 32768).astype(jnp.int16)


def decode(codes, top):
    root = (codes.astype(jnp.int32).astype(f32) + f32(32768.0)) * f32(top**0.125 / 65535.0)
    square = root * root
    fourth = square * square
    return fourth * fourth


def first_round(terms_hbm, levels_hbm, ids_hbm, postings_hbm, send_ref, mask_ref, query_ref, postings_ref,
                terms_ref, levels_ref, ids_ref, sems):
    pairs = [(terms_hbm, terms_ref), (levels_hbm, levels_ref), (ids_hbm, ids_ref)]
    pairs.append((postings_hbm, postings_ref))
    copies = [pltpu.make_async_copy(source, target, sems.at[i]) for i, (source, target) in enumerate(pairs)]
    for copy in copies:
        copy.start()
    copies[0].wait()
    copies[1].wait()
    copies[2].wait()
    slots, queries = terms_ref.shape
    docs, width = postings_ref.shape
    tiles = width // lanes
    spread = 8 * slots
    local = terms_ref[...] - lax.axis_index("term") * width
    tile_of = lax.shift_right_arithmetic(local, 7)
    lane_of = local & 127
    repeat = (iota((slots, spread), 0) == (iota((slots, spread), 1) & (slots - 1))).astype(f32).astype(bf16)
    stacked = jnp.concatenate([tile_of, lane_of, levels_ref[...]], axis=1).astype(f32).astype(bf16)
    wide = lax.dot_general(stacked, repeat, (((0,), (0,)), ((), ())), preferred_element_type=f32)
    own = lax.shift_right_logical(iota((8, spread), 1), 5) == iota((8, spread), 0)
    lane_ids = iota((lanes, spread), 0).astype(f32)
    for block in range(queries // 8):
        rows = slice(8 * block, 8 * block + 8)
        tile_now = wide[rows]
        lane_now = wide[queries + 8 * block : queries + 8 * block + 8]
        level_now = wide[2 * queries + 8 * block : 2 * queries + 8 * block + 8]
        lane_row = jnp.sum(jnp.where(own, lane_now, 0.0), axis=0, keepdims=True)
        level_own = jnp.where(own, level_now, 0.0)
        hot = jnp.where(lane_ids == lane_row, 1.0, 0.0).astype(bf16)
        parts = [jnp.where(tile_now == float(t), level_own, 0.0) for t in range(tiles)]
        totals = dot_nt(jnp.concatenate(parts, axis=0).astype(bf16), hot)
        for t in range(tiles):
            query_ref[rows, t * lanes : (t + 1) * lanes] = totals[8 * t : 8 * t + 8] * f32(0.01)
    place = (iota((docs, queries), 0) + lax.axis_index("doc") * docs).astype(jnp.int16)
    ids = ids_ref[...].astype(jnp.int16)
    member = ids[0:1, :] == place
    for j in range(1, ids.shape[0]):
        member = member | (ids[j : j + 1, :] == place)
    member = jnp.where(member, jnp.ones((), bf16), jnp.zeros((), bf16))
    same = jnp.where(iota((queries, queries), 0) == iota((queries, queries), 1), 1.0, 0.0).astype(bf16)
    mask = dot_nt(same, member)
    mask_ref[...] = mask.astype(bf16)
    copies[3].wait()
    scores = dot_nt(query_ref[...].astype(bf16), postings_ref[...])
    chosen = jnp.sum(scores * mask, axis=0, keepdims=True)
    tail = jnp.concatenate([chosen[:, i : i + lanes] for i in range(0, docs, lanes)], axis=0)
    tail = encode(tail, first_top)
    codes = encode(scores, first_top)
    for g in range(queries // 8):
        send_ref[g, :, 0:docs] = codes[8 * g : 8 * g + 4]
        send_ref[g, :, docs : 2 * docs] = codes[8 * g + 4 : 8 * g + 8]
        send_ref[g, :, 2 * docs :] = tail


def feedback_round(received_ref, mask_ref, postings_ref, send_ref):
    groups = received_ref.shape[0]
    docs, width = postings_ref.shape
    tail = decode(received_ref[0, :, 2 * docs :], first_top)
    for g in range(1, groups):
        tail = tail + decode(received_ref[g, :, 2 * docs :], first_top)
    weight = jnp.concatenate([tail[i : i + 1] for i in range(docs // lanes)], axis=1)
    weight = weight.astype(bf16).astype(f32)
    mixing = (mask_ref[...].astype(f32) * weight).astype(bf16)
    postings = postings_ref[...]
    numerator = jnp.dot(mixing, postings, preferred_element_type=f32)
    sums = jnp.dot(mixing, jnp.ones((docs, lanes), bf16), preferred_element_type=f32)
    high = sums.astype(bf16).astype(f32)
    lane = iota(sums.shape, 1)
    sums = jnp.where(lane == 0, high, jnp.where(lane == 1, sums - high, 0.0))
    for c in range(send_ref.shape[0]):
        rows = slice(4 * c, 4 * c + 4)
        send_ref[c, :, 0:width] = numerator[rows].astype(bf16)
        send_ref[c, :, width : width + lanes] = sums[rows].astype(bf16)


def totals(first_codes_ref, final_codes_ref, first_ref, final_ref, *, final_top):
    groups, rows, docs = final_codes_ref.shape
    folded = rows // 2
    for side in range(2):
        columns = slice(side * docs, (side + 1) * docs)
        total = decode(first_codes_ref[0, :, columns], first_top)
        for g in range(1, groups):
            total = total + decode(first_codes_ref[g, :, columns], first_top)
        first_ref[side * folded : (side + 1) * folded] = total
    total = decode(final_codes_ref[0], final_top)
    for g in range(1, groups):
        total = total + decode(final_codes_ref[g], final_top)
    final_ref[...] = total


def expand(received_ref, query_ref, out_ref):
    blocks, chunk, width = out_ref.shape
    total = received_ref[0].astype(f32)
    for d in range(1, received_ref.shape[0]):
        total = total + received_ref[d].astype(f32)
    weight = total[:, width : width + 1] + total[:, width + 1 : width + 2]
    doc = lax.axis_index("doc")
    pair = query_ref[pl.ds(pl.multiple_of(lax.shift_right_logical(doc, 1) * 8, 8), 8), :]
    mine = jnp.where((doc & 1) == 0, pair[:chunk], pair[chunk:])
    mine = (mine + expansion_weight * total[:, :width] / weight).astype(bf16)
    for d in range(blocks):
        out_ref[d] = mine


def rescore(gathered_ref, postings_ref, send_ref, rows_ref, *, final_top):
    chunk = gathered_ref.shape[1]
    for d in range(gathered_ref.shape[0]):
        rows_ref[chunk * d : chunk * d + chunk] = gathered_ref[d]
    codes = encode(dot_nt(rows_ref[...], postings_ref[...]), final_top)
    group = send_ref.shape[1]
    for g in range(send_ref.shape[0]):
        send_ref[g] = codes[group * g : group * g + group]


def per_device(postings, query_terms, query_levels, feedback_ids):
    docs, width = postings.shape
    queries = query_terms.shape[0]
    groups = lax.axis_size("term")
    blocks = lax.axis_size("doc")
    group = queries // groups
    chunk = queries // blocks
    shape = jax.ShapeDtypeStruct
    final_top = first_top + expansion_weight * 3.0 * 3.0 * 1.01 * width
    send, mask, query, postings = pl.pallas_call(
        first_round,
        out_shape=(
            shape((groups, group // 2, 2 * docs + lanes), jnp.int16),
            shape((queries, docs), bf16),
            shape((queries, width), f32),
            shape((docs, width), bf16),
        ),
        in_specs=[pl.BlockSpec(memory_space=pltpu.HBM)] * 4,
        out_specs=(VMEM,) * 4,
        scratch_shapes=[
            pltpu.VMEM(query_terms.shape[::-1], jnp.int32),
            pltpu.VMEM(query_levels.shape[::-1], jnp.int32),
            pltpu.VMEM(feedback_ids.shape[::-1], jnp.int32),
            pltpu.SemaphoreType.DMA((4,)),
        ],
        compiler_params=pltpu.CompilerParams(vmem_limit_bytes=32 << 20),
        name="first_round",
    )(*(
        pltpu.with_memory_space_constraint(x, pltpu.HBM)
        for x in (query_terms.T, query_levels.T, feedback_ids.T, postings)
    ))
    first_codes = lax.all_to_all(send, "term", 0, 0)
    send = pl.pallas_call(
        feedback_round,
        out_shape=shape((blocks, chunk, width + lanes), bf16),
        in_specs=[VMEM] * 3,
        out_specs=VMEM,
        compiler_params=pltpu.CompilerParams(vmem_limit_bytes=32 << 20),
        name="feedback_round",
    )(first_codes, mask, postings)
    received = lax.all_to_all(send, "doc", 0, 0)
    expanded = pl.pallas_call(
        expand,
        out_shape=shape((blocks, chunk, width), bf16),
        in_specs=[VMEM] * 2,
        out_specs=VMEM,
        compiler_params=pltpu.CompilerParams(vmem_limit_bytes=32 << 20),
        name="expand",
    )(received, query)
    gathered = lax.all_to_all(expanded, "doc", 0, 0)
    send = pl.pallas_call(
        functools.partial(rescore, final_top=final_top),
        out_shape=shape((groups, group, docs), jnp.int16),
        in_specs=[VMEM] * 2,
        out_specs=VMEM,
        scratch_shapes=[pltpu.VMEM((queries, width), bf16)],
        compiler_params=pltpu.CompilerParams(vmem_limit_bytes=32 << 20),
        name="rescore",
    )(gathered, postings)
    partial = lax.all_to_all(send, "term", 0, 0)
    return pl.pallas_call(
        functools.partial(totals, final_top=final_top),
        out_shape=(shape((group, docs), f32),) * 2,
        in_specs=[VMEM] * 2,
        out_specs=(VMEM,) * 2,
        compiler_params=pltpu.CompilerParams(vmem_limit_bytes=32 << 20),
        name="totals",
    )(first_codes, partial)


def solution(mesh):
    return jax.shard_map(
        per_device,
        mesh=mesh,
        in_specs=(P("doc", "term"), P(), P(), P()),
        out_specs=(P("term", "doc"), P("term", "doc")),
        check_vma=False,
    )
```

```python
import functools

import jax
import jax.numpy as jnp
from jax import lax
from jax.experimental import pallas as pl
from jax.experimental.pallas import tpu as pltpu
from jax.sharding import PartitionSpec as P

expansion_weight = 0.25
lanes = 128
first_top = 32 * 2.55 * 3.0 * 1.001
f32 = jnp.float32
bf16 = jnp.bfloat16
VMEM = pl.BlockSpec(memory_space=pltpu.VMEM)


def dot_nt(a, b):
    return lax.dot_general(a, b, (((1,), (1,)), ((), ())), preferred_element_type=f32)


def iota(shape, axis):
    return lax.broadcasted_iota(jnp.int32, shape, axis)


def encode(x, top):
    root = jnp.maximum(x * f32(1.0 / top), f32(1e-37))
    for _ in range(3):
        root = root * lax.rsqrt(root)
    return ((root * f32(65535.0) + f32(0.5)).astype(jnp.int32) - 32768).astype(jnp.int16)


def decode(codes, top):
    root = (codes.astype(jnp.int32).astype(f32) + f32(32768.0)) * f32(top**0.125 / 65535.0)
    square = root * root
    fourth = square * square
    return fourth * fourth


def first_round(terms_hbm, levels_hbm, ids_hbm, postings_hbm, send_ref, mask_ref, query_ref, postings_ref,
                terms_ref, levels_ref, ids_ref, sems):
    pairs = [(terms_hbm, terms_ref), (levels_hbm, levels_ref), (ids_hbm, ids_ref)]
    pairs.append((postings_hbm, postings_ref))
    copies = [pltpu.make_async_copy(source, target, sems.at[i]) for i, (source, target) in enumerate(pairs)]
    for copy in copies:
        copy.start()
    copies[0].wait()
    copies[1].wait()
    copies[2].wait()
    slots, queries = terms_ref.shape
    docs, width = postings_ref.shape
    tiles = width // lanes
    spread = 8 * slots
    local = terms_ref[...] - lax.axis_index("term") * width
    tile_of = lax.shift_right_arithmetic(local, 7)
    lane_of = local & 127
    repeat = (iota((slots, spread), 0) == (iota((slots, spread), 1) & (slots - 1))).astype(f32).astype(bf16)
    stacked = jnp.concatenate([tile_of, lane_of, levels_ref[...]], axis=1).astype(f32).astype(bf16)
    wide = lax.dot_general(stacked, repeat, (((0,), (0,)), ((), ())), preferred_element_type=f32)
    own = lax.shift_right_logical(iota((8, spread), 1), 5) == iota((8, spread), 0)
    lane_ids = iota((lanes, spread), 0).astype(f32).astype(bf16)
    for block in range(queries // 8):
        rows = slice(8 * block, 8 * block + 8)
        tile_now = wide[rows]
        lane_now = wide[queries + 8 * block : queries + 8 * block + 8]
        level_now = wide[2 * queries + 8 * block : 2 * queries + 8 * block + 8]
        lane_row = jnp.sum(jnp.where(own, lane_now, 0.0), axis=0, keepdims=True)
        level_own = jnp.where(own, level_now, 0.0)
        hot = jnp.where(lane_ids == lane_row.astype(bf16), jnp.ones((), bf16), jnp.zeros((), bf16))
        parts = [jnp.where(tile_now == float(t), level_own, 0.0) for t in range(tiles)]
        totals = dot_nt(jnp.concatenate(parts, axis=0).astype(bf16), hot)
        for t in range(tiles):
            query_ref[rows, t * lanes : (t + 1) * lanes] = totals[8 * t : 8 * t + 8] * f32(0.01)
    place = (iota((docs, queries), 0) + lax.axis_index("doc") * docs).astype(jnp.int16)
    ids = ids_ref[...].astype(jnp.int16)
    member = ids[0:1, :] == place
    for j in range(1, ids.shape[0]):
        member = member | (ids[j : j + 1, :] == place)
    member = jnp.where(member, jnp.ones((), bf16), jnp.zeros((), bf16))
    same = jnp.where(iota((queries, queries), 0) == iota((queries, queries), 1), 1.0, 0.0).astype(bf16)
    mask = dot_nt(same, member)
    mask_ref[...] = mask.astype(bf16)
    copies[3].wait()
    scores = dot_nt(query_ref[...].astype(bf16), postings_ref[...])
    chosen = jnp.sum(scores * mask, axis=0, keepdims=True)
    tail = jnp.concatenate([chosen[:, i : i + lanes] for i in range(0, docs, lanes)], axis=0)
    tail = encode(tail, first_top)
    codes = encode(scores, first_top)
    for g in range(queries // 8):
        send_ref[g, :, 0:docs] = codes[8 * g : 8 * g + 4]
        send_ref[g, :, docs : 2 * docs] = codes[8 * g + 4 : 8 * g + 8]
        send_ref[g, :, 2 * docs :] = tail


def feedback_round(received_ref, mask_ref, postings_ref, send_ref):
    groups = received_ref.shape[0]
    docs, width = postings_ref.shape
    tail = decode(received_ref[0, :, 2 * docs :], first_top)
    for g in range(1, groups):
        tail = tail + decode(received_ref[g, :, 2 * docs :], first_top)
    weight = jnp.concatenate([tail[i : i + 1] for i in range(docs // lanes)], axis=1)
    weight = weight.astype(bf16).astype(f32)
    mixing = (mask_ref[...].astype(f32) * weight).astype(bf16)
    postings = postings_ref[...]
    numerator = jnp.dot(mixing, postings, preferred_element_type=f32)
    sums = jnp.dot(mixing, jnp.ones((docs, lanes), bf16), preferred_element_type=f32)
    high = sums.astype(bf16).astype(f32)
    lane = iota(sums.shape, 1)
    sums = jnp.where(lane == 0, high, jnp.where(lane == 1, sums - high, 0.0))
    for c in range(send_ref.shape[0]):
        rows = slice(4 * c, 4 * c + 4)
        send_ref[c, :, 0:width] = numerator[rows].astype(bf16)
        send_ref[c, :, width : width + lanes] = sums[rows].astype(bf16)


def totals(first_codes_ref, final_codes_ref, first_ref, final_ref, *, final_top):
    groups, rows, docs = final_codes_ref.shape
    folded = rows // 2
    for side in range(2):
        columns = slice(side * docs, (side + 1) * docs)
        total = decode(first_codes_ref[0, :, columns], first_top)
        for g in range(1, groups):
            total = total + decode(first_codes_ref[g, :, columns], first_top)
        first_ref[side * folded : (side + 1) * folded] = total
    total = decode(final_codes_ref[0], final_top)
    for g in range(1, groups):
        total = total + decode(final_codes_ref[g], final_top)
    final_ref[...] = total


def expand(received_ref, query_ref, out_ref):
    blocks, chunk, width = out_ref.shape
    total = received_ref[0].astype(f32)
    for d in range(1, received_ref.shape[0]):
        total = total + received_ref[d].astype(f32)
    weight = total[:, width : width + 1] + total[:, width + 1 : width + 2]
    doc = lax.axis_index("doc")
    pair = query_ref[pl.ds(pl.multiple_of(lax.shift_right_logical(doc, 1) * 8, 8), 8), :]
    mine = jnp.where((doc & 1) == 0, pair[:chunk], pair[chunk:])
    mine = (mine + expansion_weight * total[:, :width] / weight).astype(bf16)
    for d in range(blocks):
        out_ref[d] = mine


def rescore(gathered_ref, postings_ref, send_ref, rows_ref, *, final_top):
    chunk = gathered_ref.shape[1]
    for d in range(gathered_ref.shape[0]):
        rows_ref[chunk * d : chunk * d + chunk] = gathered_ref[d]
    codes = encode(dot_nt(rows_ref[...], postings_ref[...]), final_top)
    group = send_ref.shape[1]
    for g in range(send_ref.shape[0]):
        send_ref[g] = codes[group * g : group * g + group]


def per_device(postings, query_terms, query_levels, feedback_ids):
    docs, width = postings.shape
    queries = query_terms.shape[0]
    groups = lax.axis_size("term")
    blocks = lax.axis_size("doc")
    group = queries // groups
    chunk = queries // blocks
    shape = jax.ShapeDtypeStruct
    final_top = first_top + expansion_weight * 3.0 * 3.0 * 1.01 * width
    send, mask, query, postings = pl.pallas_call(
        first_round,
        out_shape=(
            shape((groups, group // 2, 2 * docs + lanes), jnp.int16),
            shape((queries, docs), bf16),
            shape((queries, width), f32),
            shape((docs, width), bf16),
        ),
        in_specs=[pl.BlockSpec(memory_space=pltpu.HBM)] * 4,
        out_specs=(VMEM,) * 4,
        scratch_shapes=[
            pltpu.VMEM(query_terms.shape[::-1], jnp.int32),
            pltpu.VMEM(query_levels.shape[::-1], jnp.int32),
            pltpu.VMEM(feedback_ids.shape[::-1], jnp.int32),
            pltpu.SemaphoreType.DMA((4,)),
        ],
        compiler_params=pltpu.CompilerParams(vmem_limit_bytes=32 << 20),
        name="first_round",
    )(*(
        pltpu.with_memory_space_constraint(x, pltpu.HBM)
        for x in (query_terms.T, query_levels.T, feedback_ids.T, postings)
    ))
    first_codes = lax.all_to_all(send, "term", 0, 0)
    send = pl.pallas_call(
        feedback_round,
        out_shape=shape((blocks, chunk, width + lanes), bf16),
        in_specs=[VMEM] * 3,
        out_specs=VMEM,
        compiler_params=pltpu.CompilerParams(vmem_limit_bytes=32 << 20),
        name="feedback_round",
    )(first_codes, mask, postings)
    received = lax.all_to_all(send, "doc", 0, 0)
    expanded = pl.pallas_call(
        expand,
        out_shape=shape((blocks, chunk, width), bf16),
        in_specs=[VMEM] * 2,
        out_specs=VMEM,
        compiler_params=pltpu.CompilerParams(vmem_limit_bytes=32 << 20),
        name="expand",
    )(received, query)
    gathered = lax.all_to_all(expanded, "doc", 0, 0)
    send = pl.pallas_call(
        functools.partial(rescore, final_top=final_top),
        out_shape=shape((groups, group, docs), jnp.int16),
        in_specs=[VMEM] * 2,
        out_specs=VMEM,
        scratch_shapes=[pltpu.VMEM((queries, width), bf16)],
        compiler_params=pltpu.CompilerParams(vmem_limit_bytes=32 << 20),
        name="rescore",
    )(gathered, postings)
    partial = lax.all_to_all(send, "term", 0, 0)
    return pl.pallas_call(
        functools.partial(totals, final_top=final_top),
        out_shape=(shape((group, docs), f32),) * 2,
        in_specs=[VMEM] * 2,
        out_specs=(VMEM,) * 2,
        compiler_params=pltpu.CompilerParams(vmem_limit_bytes=32 << 20),
        name="totals",
    )(first_codes, partial)


def solution(mesh):
    return jax.shard_map(
        per_device,
        mesh=mesh,
        in_specs=(P("doc", "term"), P(), P(), P()),
        out_specs=(P("term", "doc"), P("term", "doc")),
        check_vma=False,
    )
```
